32 devices in a mesh: layer: 4 (over y, x), row: 2 (over core), col: 4 (over z).
Axes of the slice: x: 2, y: 2, z: 4, core: 2. Of those that a mesh axis runs over, the one named last changes fastest.
Arguments:
- cols: int32 [64, 16], P(('row', 'col'), 'layer'), may hold values from -1 to 63, as said below
- vals: bfloat16 [64, 16, 256, 256], P(('row', 'col'), 'layer'), as said below
- outcols: int32 [64, 4], P(('row', 'col')), may hold values from -1 to 63, as said below
Outputs:
- purified: bfloat16 [64, 4, 256, 256], P(('row', 'col'), 'layer')
The draws below stay inside these ranges and needn't reach their ends.
Inputs may be any that keep to these rules, and one draw needn't show every extreme that they name: `cols`: slots 4 * l to 4 * l + 3 of block row i hold distinct block columns k with k mod 4 = l and |k - i| <= 6, or -1. Column i is always listed in row i, and k is listed in row i exactly when i is listed in row k. vals[i, s] is block (i, cols[i, s]) of a symmetric matrix: the block listed at (k, i) is the transpose of the one at (i, k). Slots holding -1 hold zeros. `outcols`: block row i lists distinct block columns j with i <= j <= i + 12, always i itself, or -1.
All inputs are finite; a program needn't handle non-finite values.
Results may differ from the reference program's by a relative error of at most 0.0085.
Values may be sent and summed in bfloat16 or wider, within the bound.
A program may use at most 64 MiB of HBM per device.

```python
import jax
import jax.numpy as jnp
from jax import lax

B = 256
W = 6
KL = 4
KO = 4
GROUPS = 4
NB = 64


def make_cols(key):
    base_key = jax.random.fold_in(key, 11)
    first_key, second_key = jax.random.split(base_key)
    regions = (NB + 7) // 8
    region = jnp.arange(NB) // 8
    limits = jax.random.randint(first_key, (regions,), 35, 100)[region]
    rolls = jax.random.randint(second_key, (NB, W), 0, 100)
    index = jnp.arange(NB)[:, None]
    offsets = jnp.arange(1, W + 1)[None, :]
    upper = (rolls < limits[:, None]) & (index + offsets < NB)
    source = jnp.clip(index - offsets, 0, NB - 1)
    lower = upper[source, offsets - 1] & (index - offsets >= 0)
    table = jnp.concatenate([lower[:, ::-1], jnp.ones((NB, 1), dtype=bool), upper], axis=1)
    group = jnp.arange(GROUPS)[None, :, None]
    step = jnp.arange(KL)[None, None, :]
    rowid = jnp.arange(NB)[:, None, None]
    start = rowid - W + jnp.mod(group - (rowid - W), GROUPS)
    column = start + step * GROUPS
    offset = column - rowid
    inside = (offset <= W) & (column >= 0) & (column < NB)
    listed = jnp.take_along_axis(table, jnp.clip(offset + W, 0, 2 * W).reshape(NB, -1), axis=1).reshape(NB, GROUPS, KL)
    chosen = jnp.where(inside & listed, column, -1)
    return chosen.reshape(NB, GROUPS * KL).astype(jnp.int32)


def block_value(key, first, distance):
    block_key = jax.random.fold_in(jax.random.fold_in(jax.random.fold_in(key, 41), first), distance)
    raw = jax.random.normal(block_key, (B, B), jnp.float32)
    raw = 0.1 * raw
    return jnp.where(distance == 0, 0.70710678 * (raw + raw.T), raw)


def draw_cols(key, part):
    return make_cols(key)


def draw_vals(key, part):
    listing = make_cols(key)

    def one_row(index):
        columns = listing[index]
        first = jnp.minimum(index, columns)
        distance = jnp.abs(columns - index)
        blocks = jax.vmap(lambda a, d: block_value(key, a, d))(jnp.clip(first, 0, NB - 1), distance)
        flipped = jnp.swapaxes(blocks, 1, 2)
        blocks = jnp.where((columns < index)[:, None, None], flipped, blocks)
        blocks = jnp.where((columns >= 0)[:, None, None], blocks, jnp.float32(0.0))
        return blocks.astype(jnp.bfloat16)
    return lax.map(one_row, jnp.arange(NB, dtype=jnp.int32))


def draw_outcols(key, part):
    score_key = jax.random.fold_in(key, 53)
    width = 2 * W + 1
    scores = jax.random.randint(score_key, (NB, width), 0, 1000) * 32 + jnp.arange(width)[None, :]
    scores = scores + jnp.where(jnp.arange(width)[None, :] == 0, 1000000, 0)
    rowid = jnp.arange(NB)[:, None]
    scores = jnp.where(rowid + jnp.arange(width)[None, :] < NB, scores, -1)
    best, picked = lax.top_k(scores, KO)
    return jnp.where(best >= 0, rowid + picked, -1).astype(jnp.int32)


def setup_inputs(seed: int = 0) -> dict:
    arg_keys = jax.random.split(jax.random.key(seed), 4)
    return {
        "cols": draw_cols(jax.random.fold_in(arg_keys[3], 71), 0),
        "vals": draw_vals(jax.random.fold_in(arg_keys[3], 71), 0),
        "outcols": draw_outcols(jax.random.fold_in(arg_keys[3], 71), 0),
    }


def reference(cols, vals, outcols):
    nrows = vals.shape[0]
    groups = cols.shape[1] // KL

    def one_row(index):
        left = vals[index].astype(jnp.float32).reshape(groups, KL, B, B)
        left_cols = cols[index].reshape(groups, KL)
        targets = outcols[index]
        where = jnp.clip(targets, 0, nrows - 1).astype(jnp.int32)
        right = vals[where].astype(jnp.float32).reshape(KO, groups, KL, B, B)
        right_cols = cols[where].reshape(KO, groups, KL)
        hits = ((left_cols[None, :, :, None] == right_cols[:, :, None, :]) & (left_cols[None, :, :, None] >= 0)).astype(jnp.float32)
        moved = jnp.einsum('ogst,ogtab->ogsab', hits, right)
        product = jnp.einsum('gsab,ogscb->ogac', left, moved)
        owned = (left_cols[None, :, :] == targets[:, None, None]).astype(jnp.float32)
        twice = 2.0 * jnp.einsum('ogs,gsab->ogab', owned, left)
        rounded = lax.optimization_barrier((twice - product).astype(jnp.bfloat16))
        total = jnp.sum(rounded.astype(jnp.float32), axis=1)
        total = jnp.where(targets[:, None, None] >= 0, total, jnp.float32(0.0))
        return total.astype(jnp.bfloat16)

    return lax.map(one_row, jnp.arange(nrows, dtype=jnp.int32))
```

```python
import functools

import jax
import jax.numpy as jnp
from jax import lax
from jax.experimental import pallas as pl
from jax.experimental.pallas import tpu as pltpu
from jax.sharding import PartitionSpec as P

W = 6
MESH = pl.DeviceIdType.MESH


def kernel(
    sizes, cols_ref, targets_ref, vals_ref, out_ref,
    pack, halo, right, part, own, recv,
    halo_send, halo_recv, part_send, part_recv,
):
    rows, slots, outs, layers, groups, fine = sizes
    far = 2 * W
    steps = -(-(rows + W) // layers)
    layer = lax.axis_index("layer")
    group = lax.axis_index("row") * fine + lax.axis_index("col")
    base = group * rows
    zero_at = rows * slots
    halo_at = zero_at + 1

    def group_id(by):
        other = (group + by + groups) % groups
        return {"row": other // fine, "col": other % fine}

    def layer_id(by):
        return {"layer": (layer + by) % layers}

    def find(row, column):
        slot = jnp.int32(0)
        hit = jnp.int32(0)
        for s in range(slots):
            same = (cols_ref[row, s] == column).astype(jnp.int32)
            slot = slot + s * same
            hit = hit + same
        return jnp.minimum(slot, slots - 1), hit

    def halo_count(q):
        count = jnp.clip(q * layers + layer - rows + W + 1, 0, far)
        return jnp.where(q * layers + layer < rows + W, count, 0)

    def halo_copy(q, t, by):
        at = q * far + t
        return pltpu.make_async_remote_copy(
            src_ref=pack.at[at], dst_ref=halo.at[at],
            send_sem=halo_send.at[at], recv_sem=halo_recv.at[at],
            device_id=group_id(-by), device_id_type=MESH,
        )

    def part_copy(row, r):
        at = (r - 1) * rows + row
        return pltpu.make_async_remote_copy(
            src_ref=part.at[at], dst_ref=recv.at[at],
            send_sem=part_send.at[at], recv_sem=part_recv.at[at],
            device_id=layer_id(r), device_id_type=MESH,
        )

    barrier = pltpu.get_barrier_semaphore()
    for by in (-2, -1, 1, 2):
        pl.semaphore_signal(barrier, inc=1, device_id=group_id(by), device_id_type=MESH)
    for r in range(1, layers):
        pl.semaphore_signal(barrier, inc=1, device_id=layer_id(r), device_id_type=MESH)
    pl.semaphore_wait(barrier, 4 + layers - 1)

    for q in range(steps):
        count = halo_count(q)
        for by in (1, 2):
            column = base + q * layers + layer - by * rows

            def send(t, carry, q=q, by=by, column=column):
                row = t - (by - 1) * rows
                slot, hit = find(row, column)
                block = vals_ref[row, slot]
                pack[q * far + t] = jnp.where(hit > 0, block, jnp.zeros_like(block))
                halo_copy(q, t, by).start()
                return carry

            lax.fori_loop((by - 1) * rows, jnp.clip(count, (by - 1) * rows, by * rows), send, 0)

    right[zero_at] = jnp.zeros(right.shape[1:], right.dtype)

    def keep(n, carry):
        right[n] = vals_ref[n // slots, n % slots]
        return carry

    lax.fori_loop(0, rows * slots, keep, 0)

    def product(row, o):
        target = targets_ref[row, o]
        there = target - base
        near = jnp.clip(there, 0, rows - 1)
        total = None
        for s in range(slots):
            column = cols_ref[row, s]
            slot, hit = find(near, column)
            local_at = jnp.where(hit > 0, near * slots + slot, zero_at)
            t = there - rows
            place = column - base
            q = (place - layer) // layers
            reach = (place >= t + rows - W) & (t < far)
            far_at = jnp.where(reach, halo_at + q * far + t, zero_at)
            at = jnp.where(there < rows, local_at, far_at)
            at = jnp.where((target >= 0) & (column >= 0), at, zero_at)
            at = jnp.clip(at, 0, right.shape[0] - 1)
            term = lax.dot_general(
                vals_ref[row, s], right[at], (((1,), (1,)), ((), ())),
                preferred_element_type=jnp.float32,
            )
            total = term if total is None else total + term
        slot, hit = find(row, target)
        mine = (hit > 0) & (target >= 0)
        block = vals_ref[row, jnp.where(mine, slot, 0)].astype(jnp.float32)
        twice = jnp.where(mine, 2.0 * block, jnp.zeros_like(block))
        return twice - total

    def one_row(row, carry):
        for r in range(1, layers):
            part[(r - 1) * rows + row] = product(row, (layer + r) % layers).astype(part.dtype)
            part_copy(row, r).start()
        own[row] = product(row, layer)
        return carry

    for q in range(steps):
        count = halo_count(q)

        def arrive(t, carry, q=q):
            halo_copy(q, t, 1).wait_recv()
            right[halo_at + q * far + t] = halo[q * far + t]
            return carry

        lax.fori_loop(0, count, arrive, 0)
        first = jnp.clip(q * layers + layer - W, 0, rows) if q else 0
        last = jnp.clip((q + 1) * layers + layer - W, 0, rows) if q < steps - 1 else rows
        lax.fori_loop(first, last, one_row, 0)

    def finish(row, carry):
        total = own[row]
        for r in range(1, layers):
            part_copy(row, r).wait_recv()
            total = total + recv[(r - 1) * rows + row].astype(jnp.float32)
        out_ref[row, 0] = total.astype(out_ref.dtype)
        return carry

    lax.fori_loop(0, rows, finish, 0)

    for q in range(steps):
        lax.fori_loop(0, halo_count(q), lambda t, c, q=q: (halo_copy(q, t, 1).wait_send(), c)[1], 0)
    for r in range(1, layers):
        lax.fori_loop(0, rows, lambda row, c, r=r: (part_copy(row, r).wait_send(), c)[1], 0)


def solution(mesh):
    layers = mesh.shape["layer"]
    fine = mesh.shape["col"]
    groups = mesh.shape["row"] * fine

    def per_device(cols, vals, outcols):
        rows, slots, size, _ = vals.shape
        outs = outcols.shape[1]
        far = 2 * W
        steps = -(-(rows + W) // layers)
        block = (size, size)
        sent = (layers - 1) * rows
        return pl.pallas_call(
            functools.partial(kernel, (rows, slots, outs, layers, groups, fine)),
            out_shape=jax.ShapeDtypeStruct((rows, outs // layers) + block, jnp.bfloat16),
            in_specs=[
                pl.BlockSpec(memory_space=pltpu.SMEM),
                pl.BlockSpec(memory_space=pltpu.SMEM),
                pl.BlockSpec(memory_space=pltpu.VMEM),
            ],
            out_specs=pl.BlockSpec(memory_space=pltpu.VMEM),
            scratch_shapes=[
                pltpu.VMEM((steps * far,) + block, jnp.bfloat16),
                pltpu.VMEM((steps * far,) + block, jnp.bfloat16),
                pltpu.VMEM((rows * slots + 1 + steps * far,) + block, jnp.bfloat16),
                pltpu.VMEM((sent,) + block, jnp.bfloat16),
                pltpu.VMEM((rows,) + block, jnp.float32),
                pltpu.VMEM((sent,) + block, jnp.bfloat16),
                pltpu.SemaphoreType.DMA((steps * far,)),
                pltpu.SemaphoreType.DMA((steps * far,)),
                pltpu.SemaphoreType.DMA((sent,)),
                pltpu.SemaphoreType.DMA((sent,)),
            ],
            compiler_params=pltpu.CompilerParams(collective_id=0, has_side_effects=True),
        )(cols, outcols, vals)

    in_specs = (
        P(("row", "col"), "layer"),
        P(("row", "col"), "layer", None, None),
        P(("row", "col"), None),
    )
    return jax.shard_map(
        per_device, mesh=mesh, in_specs=in_specs,
        out_specs=P(("row", "col"), "layer", None, None), check_vma=False,
    )
```
